32 devices in a mesh: rep: 2 (over x), ep: 16 (over z, y, core).
Axes of the slice: x: 2, y: 2, z: 4, core: 2. Of those that a mesh axis runs over, the one named last changes fastest.
Arguments:
- tokens: bfloat16 [4096, 2048], P(('rep', 'ep')), may hold values from -6 to 6
- expert_ids: int32 [4096, 2], P(('rep', 'ep')), may hold values from 0 to 15, all different within a row; in each aligned block of 128 rows (0 to 127, 128 to 255, ...) at most 20 rows name the same one
- route_weights: bfloat16 [4096, 2], P(('rep', 'ep')), may hold values from 0.099609375 to 1
- w_gate_up: bfloat16 [16, 2048, 1536], P('ep', 'rep'), may hold values from -0.125 to 0.125
- w_down: bfloat16 [16, 2048, 768], P('ep', 'rep'), may hold values from -0.21875 to 0.21875
- grad_out: bfloat16 [4096, 2048], P(('rep', 'ep')), may hold values from -1.5 to 1.5
Outputs:
- mixed: bfloat16 [4096, 2048], P(('rep', 'ep'))
- grad_tokens: bfloat16 [4096, 2048], P(('rep', 'ep'))
- grad_gate_up: bfloat16 [16, 2048, 1536], P('ep', 'rep')
- grad_down: bfloat16 [16, 2048, 768], P('ep', 'rep')
- route_grad: float32 [4096, 2], P(('rep', 'ep'))
The draws below stay inside these ranges and needn't reach their ends.
Inputs may be any that keep to these rules, and one draw needn't show every extreme that they name: `expert_ids`: each token names 2 different experts. Among the rows of one device no expert is named more than 20 times, and in every draw some device names some expert exactly 20 times.
All inputs are finite; a program needn't handle non-finite values.
Results may differ from the reference program's by a relative error of at most 0.0095.
Values may be sent and summed in bfloat16 or wider, within the bound.
No kernel may reach another device: no remote copies, remote signals or barrier semaphores. Data moves between devices by JAX's collectives and lax.ppermute only.
A program may use at most 128 MiB of HBM per device.

```python
import math
import jax
import jax.numpy as jnp
import numpy as np
from jax import lax

D = 2048
F = 768
TOPK = 2
TOK_DEV = 128
EXPERTS = 16
TOKENS = 4096
CAP = 20
N_REP = 2


def level_of(stream_key, dims, split, low, top_value):
    def one(position, blocks):
        steps = jax.random.uniform(jax.random.fold_in(jax.random.fold_in(stream_key, 6), position), (blocks,), jnp.float32, low / len(split), top_value / len(split))
        return jnp.repeat(jnp.exp(steps), dims[position] // blocks).reshape((-1,) + (1,) * (len(dims) - position - 1))

    gain = one(*split[0])
    for cut in split[1:]:
        gain = gain * one(*cut)
    return gain


def shared_out(key, own, number, rows, count, top, limit, skew):
    order = jax.random.permutation(key, count)
    crowded, common = portions_of(count, rows * top, limit, skew, True), portions_of(count, rows * top, limit, skew, False)
    places = jnp.arange(count)

    def named(sizes, rotation):
        used = int((sizes > 0).sum())
        fixed = max(1, used // 4)
        shifted = fixed + (places - fixed + rotation * (used - fixed)) % max(1, count - fixed)
        return jnp.zeros((count,), jnp.int32).at[order[jnp.where(places < fixed, places, shifted)]].set(jnp.asarray(sizes, jnp.int32))

    sizes = jnp.where(number % 4 == 0, named(crowded, number // 4), named(common, number - number // 4 - 1))
    mixed = jax.random.permutation(jax.random.fold_in(own, 3), count)
    source_of, sink = mixed[0:count // 2 * 2:2], mixed[1:count // 2 * 2:2]
    room = jnp.minimum(sizes[source_of] - 1, limit - sizes[sink]) // 2
    room = jnp.where((source_of == order[0]) | (sink == order[0]) | (sizes[sink] == 0), 0, jnp.maximum(room, 0))
    shifted = jax.random.randint(jax.random.fold_in(own, 4), (count // 2,), 0, 1 << 20) % (room + 1)
    sizes = sizes.at[source_of].add(-shifted).at[sink].add(shifted)
    members = jnp.searchsorted(jnp.cumsum(sizes), jnp.arange(rows * top), side="right").astype(jnp.int32)
    grid = members.reshape(top, rows).T
    grid = grid[jax.random.permutation(jax.random.fold_in(own, 1), rows)]
    rotation = jax.random.randint(jax.random.fold_in(own, 2), (rows, 1), 0, top)
    return jnp.take_along_axis(grid, (jnp.arange(top)[None, :] + rotation) % top, axis=1)


def portions_of(count, total, bound, skew, full):
    portions = [(1 << 20) // math.isqrt(standing ** skew) + 1 for standing in range(1, count + 1)]
    largest = bound if full else min(bound, max(-(-total // count), total * portions[0] // sum(portions)))
    least = 1 if total - largest >= count - 1 else 0
    given, spare = [largest] + [least] * (count - 1), total - largest - least * (count - 1)
    while spare > 0:
        free = [i for i in range(1, count) if given[i] < largest] or [i for i in range(1, count) if given[i] < bound]
        whole, left = sum([portions[i] for i in free]), spare
        for i in free:
            more = min(bound - given[i], max(1, left * portions[i] // whole), spare)
            given[i] = given[i] + more
            spare = spare - more
    return np.array(given)


def normal_values(stream_key, dims, scale, reach, split=(), held_as=jnp.bfloat16):
    values = jax.random.normal(stream_key, dims, jnp.float32) * scale
    if len(split) > 0:
        values = level_of(stream_key, dims, split, -0.22, 0.18) * values
    return jnp.clip(values, min=-reach, max=reach).astype(held_as)


def setup_inputs(seed: int = 0) -> dict:
    key_of = jax.random.split(jax.random.key(seed), 7)
    tokens = normal_values(key_of[0], (TOKENS, D), 1.0, 6.0, ((0, 32),))
    expert_ids_keys = jax.random.split(jax.random.fold_in(key_of[1], 1), TOKENS // TOK_DEV)
    expert_ids_turns = jax.random.permutation(jax.random.fold_in(key_of[1], 3), TOKENS // TOK_DEV)
    expert_ids = jax.vmap(lambda own, number: shared_out(jax.random.fold_in(key_of[1], 2), own, number, TOK_DEV, EXPERTS, TOPK, CAP, 2))(expert_ids_keys, expert_ids_turns).reshape((TOKENS, TOPK))
    route_weights = jnp.clip(0.099609375 + 0.9003906 * jax.random.uniform(key_of[2], (TOKENS, TOPK), jnp.float32) ** level_of(key_of[2], (TOKENS, TOPK), ((0, 32),), -0.2, 0.2), 0.099609375, 1.0).astype(jnp.bfloat16)
    w_gate_up = normal_values(key_of[3], (EXPERTS, D, 2 * F), D ** -0.5, 0.125, ((0, 16), (1, 2)))
    w_down = normal_values(key_of[4], (EXPERTS, D, F), F ** -0.5, 0.21875, ((0, 16), (1, 2)))
    grad_out = normal_values(key_of[5], (TOKENS, D), 0.25, 1.5, ((0, 32),))
    return {"tokens": tokens, "expert_ids": expert_ids, "route_weights": route_weights, "w_gate_up": w_gate_up, "w_down": w_down, "grad_out": grad_out}


def swiglu_forward(slot_rows, weight_gu, weight_down):
    hidden_size = weight_down.shape[1]
    gate_up = jnp.dot(slot_rows, weight_gu, preferred_element_type=jnp.float32)
    gate_part = gate_up[:, :hidden_size]
    up_part = gate_up[:, hidden_size:]
    activated = (gate_part * jax.nn.sigmoid(gate_part) * up_part).astype(jnp.bfloat16)
    outputs = lax.dot_general(activated, weight_down, (((1,), (1,)), ((), ())), preferred_element_type=jnp.float32).astype(jnp.bfloat16)
    return gate_up, activated, outputs


def swiglu_backward(cotangent, gate_up, weight_gu, weight_down):
    hidden_size = weight_down.shape[1]
    gate_part = gate_up[:, :hidden_size]
    up_part = gate_up[:, hidden_size:]
    grad_hidden = jnp.dot(cotangent, weight_down, preferred_element_type=jnp.float32)
    sigmoid_gate = jax.nn.sigmoid(gate_part)
    slope = sigmoid_gate * (1.0 + gate_part * (1.0 - sigmoid_gate))
    grad_gu = jnp.concatenate([grad_hidden * up_part * slope, grad_hidden * gate_part * sigmoid_gate], axis=1).astype(jnp.bfloat16)
    grad_rows = lax.dot_general(grad_gu, weight_gu, (((1,), (1,)), ((), ())), preferred_element_type=jnp.float32).astype(jnp.bfloat16)
    return grad_gu, grad_rows


def reference(tokens, expert_ids, route_weights, w_gate_up, w_down, grad_out):
    group_slots = 2 * TOK_DEV * TOPK
    assign_total = TOKENS * TOPK
    flat_ids = expert_ids.reshape(-1).astype(jnp.int32)
    one_hot = (flat_ids[:, None] == jnp.arange(EXPERTS, dtype=jnp.int32)[None, :]).astype(jnp.int32)
    running = jnp.cumsum(one_hot.reshape(N_REP, assign_total // N_REP, EXPERTS), axis=1).reshape(assign_total, EXPERTS)
    rank = jnp.sum(running * one_hot, axis=1) - 1
    group_of = jnp.arange(assign_total, dtype=jnp.int32) // (assign_total // N_REP)
    target = flat_ids * (N_REP * group_slots) + group_of * group_slots + rank
    table = jnp.full((EXPERTS * N_REP * group_slots,), assign_total, jnp.int32)
    table = table.at[target].set(jnp.arange(assign_total, dtype=jnp.int32)).reshape(EXPERTS, N_REP * group_slots)
    tokens_ext = jnp.concatenate([tokens, jnp.zeros((1, D), jnp.bfloat16)], axis=0)
    grad_ext = jnp.concatenate([grad_out, jnp.zeros((1, D), jnp.bfloat16)], axis=0)
    weight_ext = jnp.concatenate([route_weights.reshape(-1), jnp.zeros((1,), jnp.bfloat16)], axis=0)

    def per_expert(carry, inputs):
        out_assign, rows_assign = carry
        index_row, weight_gu, weight_down = inputs
        token_row = index_row // TOPK
        slot_rows = tokens_ext[token_row]
        cotangent = (weight_ext[index_row].astype(jnp.float32)[:, None] * grad_ext[token_row].astype(jnp.float32)).astype(jnp.bfloat16)
        gate_up, activated, outputs = swiglu_forward(slot_rows, weight_gu, weight_down)
        grad_gu, grad_rows = swiglu_backward(cotangent, gate_up, weight_gu, weight_down)
        out_assign = out_assign.at[index_row].set(outputs)
        rows_assign = rows_assign.at[index_row].set(grad_rows)
        part_gu = jnp.einsum("rsd,rsf->rdf", slot_rows.reshape(N_REP, group_slots, D).astype(jnp.float32), grad_gu.reshape(N_REP, group_slots, 2 * F).astype(jnp.float32))
        part_gu = lax.optimization_barrier(part_gu.astype(jnp.bfloat16))
        sum_gu = jnp.sum(part_gu.astype(jnp.float32), axis=0).astype(jnp.bfloat16)
        part_down = jnp.einsum("rsd,rsf->rdf", cotangent.reshape(N_REP, group_slots, D).astype(jnp.float32), activated.reshape(N_REP, group_slots, F).astype(jnp.float32))
        part_down = lax.optimization_barrier(part_down.astype(jnp.bfloat16))
        sum_down = jnp.sum(part_down.astype(jnp.float32), axis=0).astype(jnp.bfloat16)
        return (out_assign, rows_assign), (sum_gu, sum_down)

    initial = (jnp.zeros((assign_total + 1, D), jnp.bfloat16), jnp.zeros((assign_total + 1, D), jnp.bfloat16))
    (out_assign, rows_assign), (grad_gate_up, grad_down) = lax.scan(per_expert, initial, (table, w_gate_up, w_down))
    expert_out = out_assign[:assign_total].reshape(TOKENS, TOPK, D).astype(jnp.float32)
    mixed = jnp.sum(route_weights.astype(jnp.float32)[:, :, None] * expert_out, axis=1).astype(jnp.bfloat16)
    route_grad = jnp.sum(grad_out.astype(jnp.float32)[:, None, :] * expert_out, axis=2)
    grad_tokens = jnp.sum(rows_assign[:assign_total].reshape(TOKENS, TOPK, D).astype(jnp.float32), axis=1).astype(jnp.bfloat16)
    return mixed, grad_tokens, grad_gate_up, grad_down, route_grad
```

```python
import functools

import jax
import jax.numpy as jnp
from jax import lax
from jax.experimental import pallas as pl
from jax.experimental.pallas import tpu as pltpu
from jax.sharding import PartitionSpec as P

USE_PERMUTES = False


def slot_lanes(me_ref, ids, dims):
    n_ep, n_rep, tok_rows, capacity, stride, relative = dims
    top, width = ids.shape
    expert = lax.broadcasted_iota(jnp.int32, (n_ep, width), 0)
    hits = [(expert == ids[k : k + 1, :]) for k in range(top)]
    named = functools.reduce(jnp.logical_or, hits)
    before = lax.broadcasted_iota(jnp.int32, (width, width), 0)
    after = lax.broadcasted_iota(jnp.int32, (width, width), 1)
    earlier = jnp.logical_and(before < after, before // tok_rows == after // tok_rows)
    rank = jnp.dot(
        named.astype(jnp.bfloat16), earlier.astype(jnp.bfloat16), preferred_element_type=jnp.float32
    ).astype(jnp.int32)
    block = lax.broadcasted_iota(jnp.int32, (n_ep, width), 1) // tok_rows
    source = (me_ref[1] + n_rep - block) % n_rep
    place = (expert ^ me_ref[0] if relative else expert) * stride + source * capacity + rank
    return [jnp.sum(jnp.where(hit, place, 0), axis=0, keepdims=True) for hit in hits]


def selection(slots, n_slots, width, scales=None):
    row = lax.broadcasted_iota(jnp.int32, (n_slots, width), 0)
    total = None
    for k, slot in enumerate(slots):
        value = 1.0 if scales is None else scales[k : k + 1, :]
        part = jnp.where(row == slot, value, 0.0)
        total = part if total is None else total + part
    return total.astype(jnp.bfloat16)


def pack_body(dims, scaled, me_ref, ids_ref, scale_ref, x_ref, out_ref):
    slots = slot_lanes(me_ref, ids_ref[...], dims)
    scales = scale_ref[...] if scaled else None
    pick = selection(slots, dims[0] * dims[4], x_ref.shape[0], scales)
    out_ref[...] = jnp.dot(pick, x_ref[...], preferred_element_type=jnp.float32).astype(
        jnp.bfloat16
    )


def unpack_out_body(dims, me_ref, ids_ref, scale_ref, grad_ref, back_ref, mixed_ref, route_ref):
    slots = slot_lanes(me_ref, ids_ref[...], dims)
    width = grad_ref.shape[0]
    pick = selection(slots, dims[0] * dims[4], width, scale_ref[...])
    mixed_ref[...] = lax.dot_general(
        pick, back_ref[...], (((0,), (0,)), ((), ())), preferred_element_type=jnp.float32
    ).astype(jnp.bfloat16)
    products = lax.dot_general(
        back_ref[...], grad_ref[...], (((1,), (1,)), ((), ())), preferred_element_type=jnp.float32
    )
    row = lax.broadcasted_iota(jnp.int32, products.shape, 0)
    for k, slot in enumerate(slots):
        route_ref[k : k + 1, :] = jnp.sum(
            jnp.where(row == slot, products, 0.0), axis=0, keepdims=True
        )


def unpack_rows_body(dims, me_ref, ids_ref, back_ref, out_ref):
    slots = slot_lanes(me_ref, ids_ref[...], dims)
    pick = selection(slots, dims[0] * dims[4], out_ref.shape[0])
    out_ref[...] = lax.dot_general(
        pick, back_ref[...], (((0,), (0,)), ((), ())), preferred_element_type=jnp.float32
    ).astype(jnp.bfloat16)


def local_call(body, name, outs, *operands):
    smem = pl.BlockSpec(memory_space=pltpu.SMEM)
    vmem = pl.BlockSpec(memory_space=pltpu.VMEM)
    return pl.pallas_call(
        body,
        out_shape=outs,
        in_specs=[smem] + [vmem] * (len(operands) - 1),
        out_specs=jax.tree.map(lambda _: vmem, outs),
        name=name,
    )(*operands)


def per_device(tokens, expert_ids, route_weights, w_gate_up, w_down, grad_out):
    n_ep, n_rep = lax.axis_size("ep"), lax.axis_size("rep")
    me, rep = lax.axis_index("ep"), lax.axis_index("rep")
    tok_rows, model_width = tokens.shape
    top = expert_ids.shape[1]
    hidden = w_down.shape[2]
    part = model_width // n_rep
    cols = hidden // n_rep
    capacity = 5 * tok_rows * top // (4 * n_ep)
    stride = -(-n_rep * capacity // 8) * 8
    n_slots = n_ep * stride
    width = n_rep * tok_rows
    f32, bf16 = jnp.float32, jnp.bfloat16

    def to_rep(x, s):
        return lax.ppermute(x, "rep", [(j, (j + s) % n_rep) for j in range(n_rep)])

    def chunk(x, s, size, axis):
        return lax.dynamic_slice_in_dim(x, (rep + s) % n_rep * size, size, axis)

    def spread(x):
        pieces = [chunk(x, 0, part, 1)] + [
            to_rep(chunk(x, s, part, 1), s) for s in range(1, n_rep)
        ]
        return jnp.concatenate(pieces, axis=0)

    def place(pieces, axis):
        size = pieces[0].shape[axis]
        shape = list(pieces[0].shape)
        shape[axis] = size * n_rep
        out = jnp.zeros(shape, pieces[0].dtype)
        for s, piece in enumerate(pieces):
            out = lax.dynamic_update_slice_in_dim(out, piece, (rep + s) % n_rep * size, axis)
        return out

    def exchange(x):
        x = x.reshape(n_ep, stride, part)
        if USE_PERMUTES:
            got = [x[0]] + [
                lax.ppermute(x[s], "ep", [(j, j ^ s) for j in range(n_ep)])
                for s in range(1, n_ep)
            ]
            return jnp.concatenate(got, axis=0)
        return lax.all_to_all(x, "ep", split_axis=0, concat_axis=0, tiled=True).reshape(
            n_slots, part
        )

    small = jnp.concatenate([expert_ids.astype(bf16), route_weights], axis=1).T
    smalls = jnp.concatenate([small] + [to_rep(small, s) for s in range(1, n_rep)], axis=1)
    ids = smalls[:top].astype(jnp.int32)
    scales = smalls[top:].astype(f32)
    me_arr = jnp.stack([me, rep]).astype(jnp.int32)
    dims = (n_ep, n_rep, tok_rows, capacity, stride, USE_PERMUTES)

    slots_shape = jax.ShapeDtypeStruct((n_slots, part), bf16)
    my_tokens = spread(tokens)
    rows_send = local_call(
        functools.partial(pack_body, dims, False), "pack_rows", slots_shape,
        me_arr, ids, scales, my_tokens,
    )
    rows = exchange(rows_send)
    my_grads = spread(grad_out)
    cot_send = local_call(
        functools.partial(pack_body, dims, True), "pack_cot", slots_shape,
        me_arr, ids, scales, my_grads,
    )
    cot = exchange(cot_send)

    gate_w = w_gate_up[0][:, :hidden]
    up_w = w_gate_up[0][:, hidden:]
    w_gu = [
        jnp.concatenate([chunk(gate_w, s, cols, 1), chunk(up_w, s, cols, 1)], axis=1)
        for s in range(n_rep)
    ]
    w_dn = [chunk(w_down[0], s, cols, 1) for s in range(n_rep)]

    def scatter_sum(x, weights):
        sent = [
            to_rep(jnp.dot(x, weights[s], preferred_element_type=f32).astype(bf16), s)
            for s in range(1, n_rep)
        ]
        total = jnp.dot(x, weights[0], preferred_element_type=f32)
        for piece in sent:
            total = total + piece.astype(f32)
        return total

    def gather(x):
        return jnp.concatenate([x] + [to_rep(x, n_rep - s) for s in range(1, n_rep)], axis=1)

    gate_up = scatter_sum(rows, w_gu)
    gate, up = gate_up[:, :cols], gate_up[:, cols:]
    sig = jax.nn.sigmoid(gate)
    act = gather((gate * sig * up).astype(bf16))
    w_dn_all = jnp.concatenate(w_dn, axis=1)
    w_gu_all = jnp.concatenate(w_gu, axis=1)
    out = lax.dot_general(
        act, w_dn_all, (((1,), (1,)), ((), ())), preferred_element_type=f32
    ).astype(bf16)
    out_back = exchange(out)

    grad_hidden = scatter_sum(cot, w_dn)
    grad_gu = gather(
        jnp.concatenate(
            [grad_hidden * up * sig * (1.0 + gate * (1.0 - sig)), grad_hidden * gate * sig], axis=1
        ).astype(bf16)
    )
    grad_rows = lax.dot_general(
        grad_gu, w_gu_all, (((1,), (1,)), ((), ())), preferred_element_type=f32
    ).astype(bf16)
    rows_back = exchange(grad_rows)

    d_down = lax.dot_general(
        cot, act, (((0,), (0,)), ((), ())), preferred_element_type=f32
    ).astype(bf16)
    d_gu = lax.dot_general(
        rows, grad_gu, (((0,), (0,)), ((), ())), preferred_element_type=f32
    ).astype(bf16)
    grad_down = place([d_down[:, s * cols : (s + 1) * cols] for s in range(n_rep)], 1)
    d_gate = [d_gu[:, 2 * s * cols : (2 * s + 1) * cols] for s in range(n_rep)]
    d_up = [d_gu[:, (2 * s + 1) * cols : (2 * s + 2) * cols] for s in range(n_rep)]
    grad_gate_up = jnp.concatenate([place(d_gate, 1), place(d_up, 1)], axis=1)

    half_shape = jax.ShapeDtypeStruct((width, part), bf16)
    mixed_part, route_part = local_call(
        functools.partial(unpack_out_body, dims), "unpack_out",
        (half_shape, jax.ShapeDtypeStruct((top, width), f32)),
        me_arr, ids, scales, my_grads, out_back,
    )
    tokens_part = local_call(
        functools.partial(unpack_rows_body, dims), "unpack_rows", half_shape,
        me_arr, ids, rows_back,
    )

    def collect(x):
        home = [x[:tok_rows]] + [
            to_rep(x[s * tok_rows : (s + 1) * tok_rows], n_rep - s) for s in range(1, n_rep)
        ]
        return place(home, 1)

    mixed = collect(mixed_part)
    grad_tokens = collect(tokens_part)
    route = route_part[:, :tok_rows]
    for s in range(1, n_rep):
        route = route + to_rep(route_part[:, s * tok_rows : (s + 1) * tok_rows], n_rep - s)
    return (mixed, grad_tokens, grad_gate_up[None], grad_down[None], route.T)


def solution(mesh):
    rows = P(("rep", "ep"), None)
    weights = P("ep", "rep", None)
    return jax.shard_map(
        per_device,
        mesh=mesh,
        in_specs=(rows, rows, rows, weights, weights, rows),
        out_specs=(rows, rows, weights, weights, rows),
        check_vma=False,
    )
```

```python
import functools

import jax
import jax.numpy as jnp
from jax import lax
from jax.experimental import pallas as pl
from jax.experimental.pallas import tpu as pltpu
from jax.sharding import PartitionSpec as P

USE_PERMUTES = False


def slot_lanes(me_ref, ids, dims):
    n_ep, n_rep, tok_rows, capacity, stride, relative = dims
    top, width = ids.shape
    expert = lax.broadcasted_iota(jnp.int32, (n_ep, width), 0)
    hits = [(expert == ids[k : k + 1, :]) for k in range(top)]
    named = functools.reduce(jnp.logical_or, hits)
    before = lax.broadcasted_iota(jnp.int32, (width, width), 0)
    after = lax.broadcasted_iota(jnp.int32, (width, width), 1)
    earlier = jnp.logical_and(before < after, before // tok_rows == after // tok_rows)
    rank = jnp.dot(
        named.astype(jnp.bfloat16), earlier.astype(jnp.bfloat16), preferred_element_type=jnp.float32
    ).astype(jnp.int32)
    block = lax.broadcasted_iota(jnp.int32, (n_ep, width), 1) // tok_rows
    source = (me_ref[1] + n_rep - block) % n_rep
    place = (expert ^ me_ref[0] if relative else expert) * stride + source * capacity + rank
    return [jnp.sum(jnp.where(hit, place, 0), axis=0, keepdims=True) for hit in hits]


def selection(slots, n_slots, width, scales=None):
    row = lax.broadcasted_iota(jnp.int32, (n_slots, width), 0)
    total = None
    for k, slot in enumerate(slots):
        value = 1.0 if scales is None else scales[k : k + 1, :]
        part = jnp.where(row == slot, value, 0.0)
        total = part if total is None else total + part
    return total.astype(jnp.bfloat16)


def pack_body(dims, scaled, me_ref, ids_ref, scale_ref, x_ref, out_ref):
    slots = slot_lanes(me_ref, ids_ref[...], dims)
    scales = scale_ref[...] if scaled else None
    pick = selection(slots, dims[0] * dims[4], x_ref.shape[0], scales)
    out_ref[...] = jnp.dot(pick, x_ref[...], preferred_element_type=jnp.float32).astype(
        jnp.bfloat16
    )


def unpack_out_body(dims, me_ref, ids_ref, scale_ref, grad_ref, back_ref, mixed_ref, route_ref):
    slots = slot_lanes(me_ref, ids_ref[...], dims)
    width = grad_ref.shape[0]
    pick = selection(slots, dims[0] * dims[4], width, scale_ref[...])
    mixed_ref[...] = lax.dot_general(
        pick, back_ref[...], (((0,), (0,)), ((), ())), preferred_element_type=jnp.float32
    ).astype(jnp.bfloat16)
    products = lax.dot_general(
        back_ref[...], grad_ref[...], (((1,), (1,)), ((), ())), preferred_element_type=jnp.float32
    )
    row = lax.broadcasted_iota(jnp.int32, products.shape, 0)
    for k, slot in enumerate(slots):
        route_ref[k : k + 1, :] = jnp.sum(
            jnp.where(row == slot, products, 0.0), axis=0, keepdims=True
        )


def unpack_rows_body(dims, me_ref, ids_ref, back_ref, out_ref):
    slots = slot_lanes(me_ref, ids_ref[...], dims)
    pick = selection(slots, dims[0] * dims[4], out_ref.shape[0])
    out_ref[...] = lax.dot_general(
        pick, back_ref[...], (((0,), (0,)), ((), ())), preferred_element_type=jnp.float32
    ).astype(jnp.bfloat16)


def local_call(body, name, outs, *operands):
    smem = pl.BlockSpec(memory_space=pltpu.SMEM)
    vmem = pl.BlockSpec(memory_space=pltpu.VMEM)
    return pl.pallas_call(
        body,
        out_shape=outs,
        in_specs=[smem] + [vmem] * (len(operands) - 1),
        out_specs=jax.tree.map(lambda _: vmem, outs),
        name=name,
    )(*operands)


def per_device(tokens, expert_ids, route_weights, w_gate_up, w_down, grad_out):
    n_ep, n_rep = lax.axis_size("ep"), lax.axis_size("rep")
    me, rep = lax.axis_index("ep"), lax.axis_index("rep")
    tok_rows, model_width = tokens.shape
    top = expert_ids.shape[1]
    hidden = w_down.shape[2]
    part = model_width // n_rep
    cols = hidden // n_rep
    capacity = 5 * tok_rows * top // (4 * n_ep)
    stride = -(-n_rep * capacity // 8) * 8
    n_slots = n_ep * stride
    width = n_rep * tok_rows
    f32, bf16 = jnp.float32, jnp.bfloat16

    def to_rep(x, s):
        return lax.ppermute(x, "rep", [(j, (j + s) % n_rep) for j in range(n_rep)])

    def chunk(x, s, size, axis):
        return lax.dynamic_slice_in_dim(x, (rep + s) % n_rep * size, size, axis)

    def spread(x):
        pieces = [chunk(x, 0, part, 1)] + [
            to_rep(chunk(x, s, part, 1), s) for s in range(1, n_rep)
        ]
        return jnp.concatenate(pieces, axis=0)

    def place(pieces, axis):
        size = pieces[0].shape[axis]
        shape = list(pieces[0].shape)
        shape[axis] = size * n_rep
        out = jnp.zeros(shape, pieces[0].dtype)
        for s, piece in enumerate(pieces):
            out = lax.dynamic_update_slice_in_dim(out, piece, (rep + s) % n_rep * size, axis)
        return out

    def exchange(x):
        x = x.reshape(n_ep, stride, part)
        if USE_PERMUTES:
            got = [x[0]] + [
                lax.ppermute(x[s], "ep", [(j, j ^ s) for j in range(n_ep)])
                for s in range(1, n_ep)
            ]
            return jnp.concatenate(got, axis=0)
        return lax.all_to_all(x, "ep", split_axis=0, concat_axis=0, tiled=True).reshape(
            n_slots, part
        )

    small = jnp.concatenate([expert_ids.astype(bf16), route_weights], axis=1).T
    smalls = jnp.concatenate([small] + [to_rep(small, s) for s in range(1, n_rep)], axis=1)
    ids = smalls[:top].astype(jnp.int32)
    scales = smalls[top:].astype(f32)
    me_arr = jnp.stack([me, rep]).astype(jnp.int32)
    dims = (n_ep, n_rep, tok_rows, capacity, stride, USE_PERMUTES)

    slots_shape = jax.ShapeDtypeStruct((n_slots, part), bf16)
    my_tokens = spread(tokens)
    rows_send = local_call(
        functools.partial(pack_body, dims, False), "pack_rows", slots_shape,
        me_arr, ids, scales, my_tokens,
    )
    rows = exchange(rows_send)
    my_grads = spread(grad_out)
    cot_send = local_call(
        functools.partial(pack_body, dims, True), "pack_cot", slots_shape,
        me_arr, ids, scales, my_grads,
    )
    cot = exchange(cot_send)

    gate_w = w_gate_up[0][:, :hidden]
    up_w = w_gate_up[0][:, hidden:]
    w_gu = [
        jnp.concatenate([chunk(gate_w, s, cols, 1), chunk(up_w, s, cols, 1)], axis=1)
        for s in range(n_rep)
    ]
    w_dn = [chunk(w_down[0], s, cols, 1) for s in range(n_rep)]

    def scatter_sum(x, weights):
        sent = [
            to_rep(jnp.dot(x, weights[s], preferred_element_type=f32).astype(bf16), s)
            for s in range(1, n_rep)
        ]
        total = jnp.dot(x, weights[0], preferred_element_type=f32)
        for piece in sent:
            total = total + piece.astype(f32)
        return total

    def gather(x):
        return jnp.concatenate([x] + [to_rep(x, n_rep - s) for s in range(1, n_rep)], axis=1)

    gate_up = scatter_sum(rows, w_gu)
    gate, up = gate_up[:, :cols], gate_up[:, cols:]
    sig = jax.nn.sigmoid(gate)
    act, gate_up = lax.optimization_barrier(((gate * sig * up).astype(bf16), gate_up))
    gate, up = gate_up[:, :cols], gate_up[:, cols:]
    sig = jax.nn.sigmoid(gate)
    act = gather(act)
    w_dn_all = jnp.concatenate(w_dn, axis=1)
    w_gu_all = jnp.concatenate(w_gu, axis=1)
    out = lax.dot_general(
        act, w_dn_all, (((1,), (1,)), ((), ())), preferred_element_type=f32
    ).astype(bf16)
    out_back = exchange(out)

    grad_hidden = scatter_sum(cot, w_dn)
    grad_gu = gather(
        jnp.concatenate(
            [grad_hidden * up * sig * (1.0 + gate * (1.0 - sig)), grad_hidden * gate * sig], axis=1
        ).astype(bf16)
    )
    grad_rows = lax.dot_general(
        grad_gu, w_gu_all, (((1,), (1,)), ((), ())), preferred_element_type=f32
    ).astype(bf16)
    rows_back = exchange(grad_rows)

    d_down = lax.dot_general(
        cot, act, (((0,), (0,)), ((), ())), preferred_element_type=f32
    ).astype(bf16)
    d_gu = lax.dot_general(
        rows, grad_gu, (((0,), (0,)), ((), ())), preferred_element_type=f32
    ).astype(bf16)
    grad_down = place([d_down[:, s * cols : (s + 1) * cols] for s in range(n_rep)], 1)
    d_gate = [d_gu[:, 2 * s * cols : (2 * s + 1) * cols] for s in range(n_rep)]
    d_up = [d_gu[:, (2 * s + 1) * cols : (2 * s + 2) * cols] for s in range(n_rep)]
    grad_gate_up = jnp.concatenate([place(d_gate, 1), place(d_up, 1)], axis=1)

    half_shape = jax.ShapeDtypeStruct((width, part), bf16)
    mixed_part, route_part = local_call(
        functools.partial(unpack_out_body, dims), "unpack_out",
        (half_shape, jax.ShapeDtypeStruct((top, width), f32)),
        me_arr, ids, scales, my_grads, out_back,
    )
    tokens_part = local_call(
        functools.partial(unpack_rows_body, dims), "unpack_rows", half_shape,
        me_arr, ids, rows_back,
    )

    def collect(x):
        home = [x[:tok_rows]] + [
            to_rep(x[s * tok_rows : (s + 1) * tok_rows], n_rep - s) for s in range(1, n_rep)
        ]
        return place(home, 1)

    mixed = collect(mixed_part)
    grad_tokens = collect(tokens_part)
    route = route_part[:, :tok_rows]
    for s in range(1, n_rep):
        route = route + to_rep(route_part[:, s * tok_rows : (s + 1) * tok_rows], n_rep - s)
    return (mixed, grad_tokens, grad_gate_up[None], grad_down[None], route.T)


def solution(mesh):
    rows = P(("rep", "ep"), None)
    weights = P("ep", "rep", None)
    return jax.shard_map(
        per_device,
        mesh=mesh,
        in_specs=(rows, rows, rows, weights, weights, rows),
        out_specs=(rows, rows, weights, weights, rows),
        check_vma=False,
    )
```

```python
import functools

import jax
import jax.numpy as jnp
from jax import lax
from jax.experimental import pallas as pl
from jax.experimental.pallas import tpu as pltpu
from jax.sharding import PartitionSpec as P


CORES = 2

STAGES = (
    "take_rows0",
    "make_act0",
    "take_rows1",
    "make_out0",
    "take_cots0",
    "make_act1",
    "make_grad_gu0",
    "make_out1",
    "take_cots1",
    "make_grad_rows0",
    "make_grad_gu1",
    "make_grad_rows1",
)


def plan_body(dims, me_ref, ids_ref, scale_ref, slot_ref, pick_ref, scaled_ref):
    order, n_rep, tok_rows, capacity, stride = dims
    chips = len(order)
    top, width = ids_ref.shape
    chip = lax.broadcasted_iota(jnp.int32, (chips, width), 0)
    hits = [chip * CORES + me_ref[1] == ids_ref[k : k + 1, :] for k in range(top)]
    named = functools.reduce(jnp.logical_or, hits)
    before = lax.broadcasted_iota(jnp.int32, (width, width), 0)
    after = lax.broadcasted_iota(jnp.int32, (width, width), 1)
    earlier = jnp.logical_and(before < after, before // tok_rows == after // tok_rows)
    rank = jnp.dot(
        named.astype(jnp.bfloat16), earlier.astype(jnp.bfloat16), preferred_element_type=jnp.float32
    ).astype(jnp.int32)
    block = lax.broadcasted_iota(jnp.int32, (chips, width), 1) // tok_rows
    source = (me_ref[2] + n_rep - block % n_rep) % n_rep * CORES + block // n_rep
    distance = chip ^ me_ref[0]
    position = jnp.zeros_like(distance)
    for i, s in enumerate(order):
        position = jnp.where(distance == s, i, position)
    place = position * stride + source * capacity + rank
    row = lax.broadcasted_iota(jnp.int32, (chips * stride, width), 0)
    pick = jnp.zeros((chips * stride, width), jnp.float32)
    scaled = jnp.zeros((chips * stride, width), jnp.float32)
    for k, hit in enumerate(hits):
        slot = jnp.sum(jnp.where(hit, place + 1, 0), axis=0, keepdims=True) - 1
        slot_ref[k : k + 1, :] = slot
        match = row == slot
        pick = jnp.where(match, 1.0, pick)
        scaled = jnp.where(match, scale_ref[k : k + 1, :], scaled)
    pick_ref[...] = pick.astype(jnp.bfloat16)
    scaled_ref[...] = scaled.astype(jnp.bfloat16)


def route_body(slot_ref, grad_ref, *refs):
    route_ref = refs[-1]
    base = 0
    sums = [0.0] * slot_ref.shape[0]
    for back_ref in refs[:-1]:
        products = lax.dot_general(
            back_ref[...],
            grad_ref[...],
            (((1,), (1,)), ((), ())),
            preferred_element_type=jnp.float32,
        )
        row = lax.broadcasted_iota(jnp.int32, products.shape, 0) + base
        base += back_ref.shape[0]
        for k in range(slot_ref.shape[0]):
            sums[k] += jnp.sum(
                jnp.where(row == slot_ref[k : k + 1, :], products, 0.0), axis=0, keepdims=True
            )
    for k, total in enumerate(sums):
        route_ref[k : k + 1, :] = total


def layer(tokens, expert_ids, route_weights, w_gate_up, w_down, grad_out):
    n_ep, n_rep = lax.axis_size("ep"), lax.axis_size("rep")
    me, rep = lax.axis_index("ep"), lax.axis_index("rep")
    tok_rows, model_width = tokens.shape
    top = expert_ids.shape[1]
    hidden = w_down.shape[2]
    part = model_width // n_rep
    cols = hidden // n_rep
    chips = n_ep // CORES
    capacity = 5 * tok_rows * top // (4 * n_ep)
    stride = n_rep * CORES * capacity
    n_slots = chips * stride
    width = n_rep * CORES * tok_rows
    half = n_rep * tok_rows
    f32, bf16 = jnp.float32, jnp.bfloat16
    if chips & (chips - 1) or stride % 8:
        raise ValueError("unsupported mesh")

    far, near = list(range(chips - 1, chips // 2 - 1, -1)), list(range(chips // 2 - 1, 0, -1))
    quarter = max(1, chips // 4)
    groups = [
        [0] + far[:quarter] + near[: quarter - 1],
        far[quarter:] + near[quarter - 1 :],
    ]
    order = groups[0] + groups[1]

    def to_rep(x, s):
        return lax.ppermute(x, "rep", [(j, (j + s) % n_rep) for j in range(n_rep)])

    def to_mate(x):
        return lax.ppermute(x, "ep", [(j, j ^ 1) for j in range(n_ep)])

    def to_chip(x, s):
        if s == 0:
            return x
        return lax.ppermute(x, "ep", [(j, j ^ (CORES * s)) for j in range(n_ep)])

    def chunk(x, s, size, axis):
        return lax.dynamic_slice_in_dim(x, (rep + s) % n_rep * size, size, axis)

    def absolute(pieces, axis):
        return jnp.concatenate(
            [lax.select_n((q - rep) % n_rep, *pieces) for q in range(n_rep)], axis=axis
        )

    def share(pieces, axis):
        return jnp.concatenate(list(pieces) + [to_mate(x) for x in pieces], axis=axis)

    def spread(x):
        return share(
            [chunk(x, 0, part, 1)]
            + [to_rep(chunk(x, s, part, 1), s) for s in range(1, n_rep)],
            0,
        )

    small = jnp.concatenate([expert_ids.astype(bf16), route_weights], axis=1).T
    smalls = share([small] + [to_rep(small, s) for s in range(1, n_rep)], 1)
    ids = smalls[:top].astype(jnp.int32)
    scales = smalls[top:].astype(f32)
    where_am_i = jnp.stack([me // CORES, me % CORES, rep]).astype(jnp.int32)

    smem = pl.BlockSpec(memory_space=pltpu.SMEM)
    vmem = pl.BlockSpec(memory_space=pltpu.VMEM)
    pick_shape = jax.ShapeDtypeStruct((n_slots, width), bf16)
    slots, pick, scaled = pl.pallas_call(
        functools.partial(plan_body, (order, n_rep, tok_rows, capacity, stride)),
        out_shape=(jax.ShapeDtypeStruct((top, width), jnp.int32), pick_shape, pick_shape),
        in_specs=[smem, vmem, vmem],
        out_specs=(vmem, vmem, vmem),
        name="plan",
    )(where_am_i, ids, scales)

    last = [where_am_i]
    sizes = [len(group) * stride for group in groups]
    starts = [0, sizes[0]]

    def gate(values):
        return lax.optimization_barrier((values, last[0]))[0]

    def mark(x):
        last[0] = x

    def blocks_of(x, k):
        return [x[i * stride : (i + 1) * stride] for i in range(len(groups[k]))]

    def send(blocks, k):
        return [to_chip(x, s) for x, s in zip(blocks, groups[k])]

    def pack(selection, x, k):
        part_of = selection[starts[k] : starts[k] + sizes[k]]
        return blocks_of(jnp.dot(part_of, x, preferred_element_type=f32).astype(bf16), k)

    def matmul(x, w):
        return jnp.dot(x, w, preferred_element_type=f32)

    def matmul_t(x, w):
        return lax.dot_general(x, w, (((1,), (1,)), ((), ())), preferred_element_type=f32)

    def start_sum(x, weights):
        parts = [matmul(x, weights[s]).astype(bf16) for s in range(1, n_rep)]
        mark(parts[-1])
        return [to_rep(p, s + 1) for s, p in enumerate(parts)]

    def finish_sum(kept, sent):
        for piece in sent:
            kept = kept + piece.astype(f32)
        return kept

    def start_gather(x):
        mark(x)
        return [to_rep(x, n_rep - s) for s in range(1, n_rep)]

    my_tokens = spread(tokens)
    in_flight = []
    for k in range(2):
        packed = pack(pick, my_tokens, k)
        in_flight.append(send(packed, k))
        mark(packed[-1])

    grad_out, w_gu_full, w_dn_full = gate((grad_out, w_gate_up[0], w_down[0]))
    my_grads = spread(grad_out)
    packed_cots = [pack(scaled, my_grads, k) for k in range(2)]
    w_gu = [
        jnp.concatenate(
            [chunk(w_gu_full[:, :hidden], s, cols, 1), chunk(w_gu_full[:, hidden:], s, cols, 1)],
            axis=1,
        )
        for s in range(n_rep)
    ]
    w_dn = [chunk(w_dn_full, s, cols, 1) for s in range(n_rep)]
    packed_cots, w_gu, w_dn = lax.optimization_barrier((packed_cots, w_gu, w_dn))
    mark(packed_cots[1][-1])

    rows, cots, acts, grads_gu = [None] * 2, [None] * 2, [None] * 2, [None] * 2
    cot_flight, out_flight, row_flight = [None] * 2, [None] * 2, [None] * 2
    sums, act_flight, ggu_flight = {}, {}, {}
    gate_ups = [None] * 2

    def take_rows(k):
        blocks, to_send = gate((in_flight[k], packed_cots[k]))
        rows[k] = jnp.concatenate(blocks, axis=0)
        sums["gu", k] = start_sum(rows[k], w_gu)
        cot_flight[k] = send(to_send, k)

    def make_act(k):
        sent, x = gate((sums["gu", k], rows[k]))
        gate_up = finish_sum(matmul(x, w_gu[0]), sent)
        gate_part, up_part = gate_up[:, :cols], gate_up[:, cols:]
        act = (gate_part * jax.nn.sigmoid(gate_part) * up_part).astype(bf16)
        act, gate_ups[k] = lax.optimization_barrier((act, gate_up))
        act_flight[k] = (act, start_gather(act))

    def make_out(k):
        own, others = act_flight[k]
        others = gate(others)
        acts[k] = absolute([own] + others, 1)
        blocks = blocks_of(matmul_t(acts[k], w_dn_full).astype(bf16), k)
        mark(blocks[-1])
        out_flight[k] = send(blocks, k)

    def take_cots(k):
        cots[k] = jnp.concatenate(gate(cot_flight[k]), axis=0)
        sums["gh", k] = start_sum(cots[k], w_dn)

    def make_grad_gu(k):
        sent, x = gate((sums["gh", k], cots[k]))
        grad_hidden = finish_sum(matmul(x, w_dn[0]), sent)
        gate_part, up_part = gate_ups[k][:, :cols], gate_ups[k][:, cols:]
        sig = jax.nn.sigmoid(gate_part)
        grad_gu = jnp.concatenate(
            [
                grad_hidden * up_part * sig * (1.0 + gate_part * (1.0 - sig)),
                grad_hidden * gate_part * sig,
            ],
            axis=1,
        ).astype(bf16)
        ggu_flight[k] = (grad_gu, start_gather(grad_gu))

    def make_grad_rows(k):
        own, others = ggu_flight[k]
        pieces = [own] + gate(others)
        grads_gu[k] = jnp.concatenate(
            [absolute([p[:, :cols] for p in pieces], 1), absolute([p[:, cols:] for p in pieces], 1)],
            axis=1,
        )
        blocks = blocks_of(matmul_t(grads_gu[k], w_gu_full).astype(bf16), k)
        mark(blocks[-1])
        row_flight[k] = send(blocks, k)

    stages = {
        "take_rows": take_rows,
        "make_act": make_act,
        "make_out": make_out,
        "take_cots": take_cots,
        "make_grad_gu": make_grad_gu,
        "make_grad_rows": make_grad_rows,
    }
    for name in STAGES:
        stage, k = name[:-1], int(name[-1])
        stages[stage](k)

    def outer(left, right):
        total = None
        for x, y in zip(left, right):
            one = lax.dot_general(x, y, (((0,), (0,)), ((), ())), preferred_element_type=f32)
            total = one if total is None else total + one
        return total.astype(bf16)

    out_flight, cots_late, rows_late = gate((out_flight, cots, rows))
    grad_down = outer(cots_late, acts)
    grad_gate_up = outer(rows_late, grads_gu)

    def combine(weights, backs):
        total = None
        for k, back in enumerate(backs):
            part_of = weights[starts[k] : starts[k] + sizes[k]]
            one = lax.dot_general(
                part_of, back, (((0,), (0,)), ((), ())), preferred_element_type=f32
            )
            total = one if total is None else total + one
        return total

    def collect(partial):
        sums = partial[:half] + to_mate(partial[half:].astype(bf16)).astype(f32)
        sums = sums.astype(bf16)
        home = [sums[:tok_rows]] + [
            to_rep(sums[s * tok_rows : (s + 1) * tok_rows], n_rep - s) for s in range(1, n_rep)
        ]
        return absolute(home, 1)

    backs = [jnp.concatenate(blocks, axis=0) for blocks in out_flight]
    mixed = collect(combine(scaled, backs))
    route_part = pl.pallas_call(
        route_body,
        out_shape=jax.ShapeDtypeStruct((top, width), f32),
        in_specs=[vmem, vmem] + [vmem] * len(backs),
        out_specs=vmem,
        name="route",
    )(slots, my_grads, *backs)
    route_part = route_part[:, :half] + to_mate(route_part[:, half:])
    route = route_part[:, :tok_rows]
    for s in range(1, n_rep):
        route = route + to_rep(route_part[:, s * tok_rows : (s + 1) * tok_rows], n_rep - s)
    grad_tokens = collect(
        combine(pick, [jnp.concatenate(blocks, axis=0) for blocks in row_flight])
    )
    return (mixed, grad_tokens, grad_gate_up[None], grad_down[None], route.T)


def solution(mesh):
    rows = P(("rep", "ep"), None)
    weights = P("ep", "rep", None)
    return jax.shard_map(
        layer,
        mesh=mesh,
        in_specs=(rows, rows, rows, weights, weights, rows),
        out_specs=(rows, rows, weights, weights, rows),
        check_vma=False,
    )
```
